32 devices in a mesh: ctx: 8 (over z, x), ch: 4 (over y, core).
Axes of the slice: x: 2, y: 2, z: 4, core: 2. Of those that a mesh axis runs over, the one named last changes fastest.
Arguments:
- signal: float32 [64, 65536], P('ch', 'ctx'), parts along dimension 0, may hold values from -6 to 6
- gate: float32 [64, 65536], P('ch', 'ctx'), parts along dimension 0, may hold values from -6 to 6
- skip: float32 [64], P('ch'), parts along dimension 0, may hold values from 0.5 to 1.5
- filter_spectrum: float32 [16, 2, 64, 8192], P('ctx', None, 'ch'), parts along dimension 2, may hold values from -6 to 6
Outputs:
- gated: float32 [64, 65536], P('ch', 'ctx'), parts along dimension 0
The draws below stay inside these ranges and needn't reach their ends.
There are 4 independent parts, one for each index of `ch`. The reference program is written for one: setup_inputs(seed, part) draws one part's arguments, and reference() takes and returns one part's arrays. A program takes and returns all parts, laid end to end along the dimension named above; each array names one. Nothing has to cross between parts.
All inputs are finite; a program needn't handle non-finite values.
Results may differ from the reference program's by a relative error of at most 0.00005.
Values sent between devices are 32-bit elements; how exact they have to be, the bound alone decides.
No kernel may reach another device: no remote copies, remote signals or barrier semaphores. Data moves between devices by JAX's collectives and lax.ppermute only.
A program may use at most 128 MiB of HBM per device.

```python
import jax
import jax.numpy as jnp

CH = 16
TOK_DEV = 8192
TOKENS = 65536
N_CTX = 8


def block_scale(own_key, shape, pieces, least, top_value):
    loudness, own = 1.0, jax.random.fold_in(own_key, 6)
    for position, blocks in pieces:
        steps = jnp.exp(jax.random.uniform(jax.random.fold_in(own, position), (blocks,), jnp.float32, least / len(pieces), top_value / len(pieces)))
        loudness = loudness * jnp.repeat(steps, shape[position] // blocks).reshape([-1 if axis == position else 1 for axis in range(len(shape))])
    return loudness


def centred(own_key, extent, spread, limit, shards=(), kind=jnp.bfloat16):
    result = spread * jax.random.normal(own_key, extent, jnp.float32)
    if shards:
        result = result * block_scale(own_key, extent, shards, -0.22, 0.18)
    return jnp.clip(result, -limit, limit).astype(kind)


def setup_inputs(seed: int = 0, part: int = 0) -> dict:
    arg_keys = jax.random.split(jax.random.key(seed), 5)
    own_keys = jax.random.split(jax.random.fold_in(arg_keys[4], part), 5)
    signal = centred(own_keys[0], (CH, TOKENS), 1.0, 6.0, ((1, 8),), jnp.float32)
    gate = centred(own_keys[1], (CH, TOKENS), 1.0, 6.0, ((1, 8),), jnp.float32)
    skip = jnp.clip(jax.random.uniform(own_keys[2], (CH,), jnp.float32, 0.5, 1.5), 0.5, 1.5)
    filter_spectrum = centred(own_keys[3], (2 * N_CTX, 2, CH, TOK_DEV), 1.0, 6.0, ((0, 8),), jnp.float32)
    return {"signal": signal, "gate": gate, "skip": skip, "filter_spectrum": filter_spectrum}


def reference(signal, gate, skip, filter_spectrum):
    freq_rows = 2 * N_CTX
    full_len = 2 * TOKENS
    padded = jnp.concatenate([signal, jnp.zeros_like(signal)], axis=1)
    spectrum = jnp.fft.fft(padded, axis=1)
    low_freq = jnp.arange(freq_rows, dtype=jnp.int32)
    mirror_row = 2 * (freq_rows - low_freq) + 1
    row_index = jnp.where(low_freq == 0, 0, jnp.where(low_freq == N_CTX, 1, jnp.where(low_freq < N_CTX, 2 * low_freq, mirror_row)))
    row_index = jnp.clip(row_index, 0, freq_rows - 1).astype(jnp.int32)
    table = filter_spectrum[row_index]
    table = jnp.transpose(table, (1, 2, 3, 0)).reshape(2, CH, full_len)
    filt = table[0] + 1j * table[1]
    product = spectrum * filt
    convolved = jnp.real(jnp.fft.ifft(product, axis=1))[:, :TOKENS]
    return gate * (convolved + skip[:, None] * signal)
```

```python
import functools
import math

import jax
import jax.numpy as jnp
import numpy as np
from jax import lax
from jax.experimental import pallas as pl
from jax.experimental.pallas import tpu as pltpu
from jax.sharding import PartitionSpec as P

LANES = 128
HALF = LANES // 2


def split_pair(values):
    high = values.astype(jnp.bfloat16)
    low = (values - high.astype(jnp.float32)).astype(jnp.bfloat16)
    return high, low


def split_table(table):
    table = np.asarray(table, np.float32)
    high = table.astype(jnp.bfloat16)
    low = (table - high.astype(np.float32)).astype(jnp.bfloat16)
    return np.stack([high, low])


def multiply(left, right, dims):
    def dot(a, b):
        return lax.dot_general(a, b, (dims, ((), ())), preferred_element_type=jnp.float32)

    return dot(left[0], right[0]) + (dot(left[0], right[1]) + dot(left[1], right[0]))


ROWS_COLS = ((1,), (0,))
COLS_COLS = ((0,), (0,))


@functools.lru_cache(maxsize=None)
def tables(parts, blocks):
    freq_rows = 2 * parts
    period = freq_rows * blocks
    full_len = period * LANES
    rows = np.arange(parts * blocks)
    index = np.zeros((parts, blocks), np.int64)
    for owner in range(parts):
        for place in range(blocks):
            if owner:
                index[owner, place] = freq_rows * place + owner
            elif place < blocks // 2:
                index[owner, place] = freq_rows * place
            else:
                index[owner, place] = freq_rows * (place - blocks // 2) + parts
    index = index.reshape(-1)
    angle = 2 * np.pi * ((index[:, None] * rows[None, :]) % period) / period
    wave_re, wave_im = np.cos(angle), -np.sin(angle)
    wave_im[0] = np.where(rows % 2 == 0, 1.0, -1.0)
    outer = np.concatenate([wave_re, wave_im], axis=0)
    lane = np.arange(LANES)
    turn = 2 * np.pi * ((index[:, None] * lane[None, :]) % full_len) / full_len
    twist = np.stack([np.cos(turn), np.sin(turn)])
    twist[0, 0], twist[1, 0] = 1.0, 0.0
    freq = 2 * (lane % HALF) + lane // HALF
    theta = 2 * np.pi * ((lane[:, None] * freq[None, :]) % LANES) / LANES
    cos, sin = np.cos(theta), np.sin(theta)
    inner = np.block([[cos, -sin], [sin, cos]])
    inner_back = np.block([[cos.T, sin.T], [-sin.T, cos.T]]) / full_len
    upper = lane % HALF >= HALF // 2
    half_theta = 2 * np.pi * ((lane[:, None] * (2 * freq[None, :] + 1)) % (2 * LANES)) / (2 * LANES)
    alternate = np.where(lane % 2 == 0, 1.0, -1.0)
    zero_re, zero_im = np.where(upper, 0.0, cos), np.where(upper, 0.0, -sin)
    zero_re[:, 0], zero_im[:, 0] = 1.0, alternate
    mid_re = np.where(upper, np.cos(half_theta), 0.0)
    mid_im = np.where(upper, -np.sin(half_theta), 0.0)
    edge = np.block([[zero_re, zero_im], [mid_re, mid_im]])
    weight = np.ones(LANES)
    weight[0] = 0.5
    edge_back = np.block([[zero_re, mid_re], [zero_im, mid_im]])
    back_re = np.concatenate([(zero_re * weight).T, mid_re.T], axis=1)
    back_im = np.concatenate([(zero_im * weight).T, mid_im.T], axis=1)
    edge_back = np.concatenate([back_re, back_im], axis=0) / full_len
    return {
        "outer": split_table(outer.T),
        "twist": twist.astype(np.float32),
        "inner": split_table(inner),
        "edge": split_table(edge),
        "inner_back": split_table(inner_back),
        "edge_back": split_table(edge_back),
    }


def spread_kernel(signal_ref, out_ref):
    channels, length = signal_ref.shape
    blocks = length // LANES
    for block in range(blocks):
        out_ref[pl.ds(block, channels, stride=blocks), :] = signal_ref[:, block * LANES : (block + 1) * LANES]


def fold_kernel(device_ref, filter_ref, out_ref, work_ref):
    channels = filter_ref.shape[2]
    blocks = filter_ref.shape[3] // LANES
    lane = lax.broadcasted_iota(jnp.int32, (channels, LANES), 1)
    reverse = LANES - 1 - lane
    negate = (LANES - lane) % LANES

    def tile(row, part, block):
        return filter_ref[row, part, :, block * LANES : (block + 1) * LANES]

    def pick(values, where):
        return jnp.take_along_axis(values, where, axis=1)

    def put(part, block, values):
        work_ref[part, pl.ds(block, channels, stride=blocks), :] = values

    @pl.when(device_ref[0] != 0)
    def _():
        for block in range(blocks):
            mirror = blocks - 1 - block
            put(0, block, tile(0, 0, block) + pick(tile(1, 0, mirror), reverse))
            put(1, block, tile(0, 1, block) - pick(tile(1, 1, mirror), reverse))

    @pl.when(device_ref[0] == 0)
    def _():
        place = lane % HALF
        for block in range(blocks):
            mirror, wrapped = blocks - 1 - block, (blocks - block) % blocks
            for part in range(2):
                sign = 1.0 - 2.0 * part
                below = jnp.where(lane == 0, tile(0, part, wrapped), pick(tile(0, part, mirror), negate))
                low = tile(0, part, block) + sign * below
                high = tile(1, part, block) + sign * pick(tile(1, part, mirror), reverse)
                values = jnp.where(place < HALF // 2, low, pltpu.roll(high, HALF // 2, 1))
                if block >= blocks // 2:
                    values = jnp.where(place == 0, pltpu.roll(low, LANES - HALF // 2, 1), values)
                if block == 0 and part == 1:
                    values = jnp.where(lane == 0, 2.0 * tile(0, 0, blocks // 2), values)
                put(part, block, values)

    left = lax.broadcasted_iota(jnp.int32, (blocks, LANES), 1) < HALF
    for pair in range(channels // 2):
        for part in range(2):
            block = work_ref[part, pl.ds(pair * 2 * blocks, 2 * blocks), :]
            turned = block.T
            first, second = turned[:blocks], turned[blocks:]
            out_ref[2 * pair, part] = jnp.where(left, first, pltpu.roll(second, HALF, 1))
            out_ref[2 * pair + 1, part] = jnp.where(left, pltpu.roll(first, HALF, 1), second)


def forward_kernel(x_ref, outer_ref, twist_ref, inner_ref, edge_ref, out_ref):
    parts, own, blocks, _ = x_ref.shape
    slots = parts * blocks
    rows = jnp.concatenate(
        [jnp.concatenate([x_ref[part, c] for part in range(parts)], axis=0) for c in range(own)], axis=1
    )
    first = multiply((outer_ref[0], outer_ref[1]), split_pair(rows), COLS_COLS)
    cos, sin = twist_ref[0], twist_ref[1]
    head = lax.broadcasted_iota(jnp.int32, (8, 2 * LANES), 0) == 0
    for c in range(own):
        re = first[:slots, c * LANES : (c + 1) * LANES]
        im = first[slots:, c * LANES : (c + 1) * LANES]
        turned = jnp.concatenate([re * cos + im * sin, im * cos - re * sin], axis=1)
        pair = split_pair(turned)
        spectrum = multiply(pair, (inner_ref[0], inner_ref[1]), ROWS_COLS)
        edge = multiply((pair[0][:16], pair[1][:16]), (edge_ref[0], edge_ref[1]), ROWS_COLS)
        out_ref[c, 0] = spectrum[:, :LANES]
        out_ref[c, 1] = spectrum[:, LANES:]
        top = jnp.where(head, edge[:8], spectrum[:8])
        out_ref[c, 0, :8] = top[:, :LANES]
        out_ref[c, 1, :8] = top[:, LANES:]


def backward_kernel(spectrum_ref, filter_ref, outer_ref, twist_ref, inner_ref, edge_ref, out_ref):
    parts, own, _, blocks, _ = filter_ref.shape
    slots = parts * blocks
    cos, sin = twist_ref[0], twist_ref[1]
    row = lax.broadcasted_iota(jnp.int32, (slots, LANES), 0)
    lane = lax.broadcasted_iota(jnp.int32, (slots, LANES), 1)
    corner = jnp.logical_and(row == 0, lane == 0)
    head = lax.broadcasted_iota(jnp.int32, (8, 2 * LANES), 0) == 0
    columns = []
    for c in range(own):
        filt_re = jnp.concatenate([filter_ref[part, c, 0] for part in range(parts)], axis=0)
        filt_im = jnp.concatenate([filter_ref[part, c, 1] for part in range(parts)], axis=0)
        re, im = spectrum_ref[c, 0], spectrum_ref[c, 1]
        low, high = re * filt_re, im * filt_im
        out_re = jnp.where(corner, low, low - high)
        out_im = jnp.where(corner, high, re * filt_im + im * filt_re)
        pair = split_pair(jnp.concatenate([out_re, out_im], axis=1))
        back = multiply(pair, (inner_ref[0], inner_ref[1]), ROWS_COLS)
        edge = multiply((pair[0][:16], pair[1][:16]), (edge_ref[0], edge_ref[1]), ROWS_COLS)
        top = jnp.where(head, edge[:8], back[:8])
        back = jnp.concatenate([top, back[8:]], axis=0)
        re, im = back[:, :LANES], back[:, LANES:]
        columns.append(jnp.concatenate([re * cos - im * sin, im * cos + re * sin], axis=0))
    turned = split_pair(jnp.concatenate(columns, axis=1))
    result = multiply((outer_ref[0], outer_ref[1]), turned, ROWS_COLS)
    for part in range(parts):
        for c in range(own):
            out_ref[part, c] = result[part * blocks : (part + 1) * blocks, c * LANES : (c + 1) * LANES]


def finish_kernel(conv_ref, signal_ref, gate_ref, skip_ref, out_ref):
    channels, length = signal_ref.shape
    blocks = length // LANES
    skip = skip_ref[...]
    for block in range(blocks):
        where = slice(block * LANES, (block + 1) * LANES)
        conv = conv_ref[pl.ds(block, channels, stride=blocks), :]
        out_ref[:, where] = gate_ref[:, where] * (conv + skip * signal_ref[:, where])


def call(kernel, shape, *operands, scratch=(), smem=0):
    specs = [pl.BlockSpec(memory_space=pltpu.SMEM)] * smem
    specs += [pl.BlockSpec(memory_space=pltpu.VMEM)] * (len(operands) - smem)
    return pl.pallas_call(
        kernel,
        out_shape=jax.ShapeDtypeStruct(shape, jnp.float32),
        in_specs=specs,
        out_specs=pl.BlockSpec(memory_space=pltpu.VMEM),
        scratch_shapes=scratch,
    )(*operands)


def exchange(values):
    return lax.all_to_all(values, "ctx", split_axis=0, concat_axis=0, tiled=True)


def by_channel(signal, gate, skip, filter_spectrum):
    parts = lax.axis_size("ctx")
    channels, length = signal.shape
    blocks, own = length // LANES, channels // parts
    table = tables(parts, blocks)
    device = lax.axis_index("ctx")[None]
    spread = call(spread_kernel, (channels * blocks, LANES), signal)
    columns = exchange(spread.reshape(parts, own, blocks, LANES))
    folded = call(
        fold_kernel,
        (channels, 2, blocks, LANES),
        device,
        filter_spectrum,
        scratch=[pltpu.VMEM((2, channels * blocks, LANES), jnp.float32)],
        smem=1,
    )
    filt = exchange(folded.reshape(parts, own, 2, blocks, LANES))
    spectrum = call(
        forward_kernel,
        (own, 2, parts * blocks, LANES),
        columns,
        table["outer"],
        table["twist"],
        table["inner"],
        table["edge"],
    )
    rows = call(
        backward_kernel,
        (parts, own, blocks, LANES),
        spectrum,
        filt,
        table["outer"],
        table["twist"],
        table["inner_back"],
        table["edge_back"],
    )
    convolved = exchange(rows).reshape(channels * blocks, LANES)
    return call(finish_kernel, signal.shape, convolved, signal, gate, skip[:, None])


def contract(form, left, right):
    return jnp.einsum(form, left, right, precision=lax.Precision.HIGHEST)


def phase_table(left, right, period):
    angle = left * right % period
    theta = angle.astype(jnp.float32) * (2.0 * math.pi / period)
    return (jnp.cos(theta), jnp.sin(theta))


def product_pair(form, left, right):
    real_part = contract(form, left[0], right[0]) - contract(form, left[1], right[1])
    imag_part = contract(form, left[0], right[1]) + contract(form, left[1], right[0])
    return (real_part, imag_part)


def times_pair(left, right):
    return (left[0] * right[0] - left[1] * right[1], left[0] * right[1] + left[1] * right[0])


def local_tables(length):
    outer_len = 128
    inner_len = length // outer_len
    outer_index = jnp.arange(outer_len, dtype=jnp.int32)
    inner_index = jnp.arange(inner_len, dtype=jnp.int32)
    outer_wave = phase_table(outer_index[:, None], outer_index[None, :], outer_len)
    twist_wave = phase_table(outer_index[:, None], inner_index[None, :], length)
    inner_wave = phase_table(inner_index[:, None], inner_index[None, :], inner_len)
    return (outer_len, inner_len, outer_wave, twist_wave, inner_wave)


def local_forward(values, length):
    outer_len, inner_len, outer_wave, twist_wave, inner_wave = local_tables(length)
    lead_shape = values[0].shape[:-1]
    values = tuple((part.reshape(lead_shape + (outer_len, inner_len)) for part in values))
    values = product_pair("as,...sb->...ab", (outer_wave[0], -outer_wave[1]), values)
    values = times_pair(values, (twist_wave[0], -twist_wave[1]))
    return product_pair("...as,bs->...ab", values, (inner_wave[0], -inner_wave[1]))


def local_inverse(values, length):
    outer_len, inner_len, outer_wave, twist_wave, inner_wave = local_tables(length)
    lead_shape = values[0].shape[:-2]
    values = product_pair("...ak,sk->...as", values, inner_wave)
    values = times_pair(values, twist_wave)
    values = product_pair("ta,...as->...ts", outer_wave, values)
    return tuple((part.reshape(lead_shape + (length,)) for part in values))


def by_frequency(signal, gate, skip, filter_spectrum):
    parts_count = lax.axis_size("ctx")
    freq_rows = 2 * parts_count
    channels, tok_local = signal.shape
    slice_len = tok_local // parts_count
    full_len = freq_rows * tok_local
    device = lax.axis_index("ctx")
    is_first = device == 0
    columns = lax.all_to_all(signal[None], "ctx", split_axis=2, concat_axis=0, tiled=True)
    source_row = jnp.arange(parts_count, dtype=jnp.int32)
    dest_index = jnp.arange(parts_count, dtype=jnp.int32)
    slice_pos = device * slice_len + jnp.arange(slice_len, dtype=jnp.int32)
    upper_freq = jnp.where(dest_index == 0, parts_count, freq_rows - dest_index)
    row_freq = jnp.stack([dest_index, upper_freq], axis=1).reshape(freq_rows)
    spot = jnp.arange(tok_local, dtype=jnp.int32)
    wave_cos, wave_sin = phase_table(row_freq[:, None], source_row[None, :], freq_rows)
    first_re = contract("kr,rcq->kcq", wave_cos, columns)
    first_im = -contract("kr,rcq->kcq", wave_sin, columns)
    twist_cos, twist_sin = phase_table(row_freq[:, None], slice_pos[None, :], full_len)
    first_pair = times_pair((first_re, first_im), (twist_cos[:, None, :], -twist_sin[:, None, :]))
    stacked = jnp.stack(first_pair, axis=1)
    moved = lax.all_to_all(stacked, "ctx", split_axis=0, concat_axis=3, tiled=True)
    low_pair = (moved[0, 0], moved[0, 1])
    high_pair = (moved[1, 0], moved[1, 1])
    rows_pair = (jnp.stack([low_pair[0], high_pair[0]]), jnp.stack([low_pair[1], high_pair[1]]))
    spectral = local_forward(rows_pair, tok_local)
    inner_len = tok_local // 128
    filt = filter_spectrum.reshape(2, 2, channels, inner_len, 128).swapaxes(3, 4)
    product = times_pair(spectral, (filt[:, 0], filt[:, 1]))
    restored = local_inverse(product, tok_local)
    my_freq = jnp.stack([device, jnp.where(is_first, parts_count, freq_rows - device)])
    back_cos, back_sin = phase_table(my_freq[:, None], spot[None, :], full_len)
    turned = times_pair(restored, (back_cos[:, None, :], back_sin[:, None, :]))
    scale_factor = 1.0 / full_len
    stacked = jnp.stack(turned, axis=1)
    moved = lax.all_to_all(stacked, "ctx", split_axis=3, concat_axis=0, tiled=True)
    out_cos, out_sin = phase_table(source_row[:, None], row_freq[None, :], freq_rows)
    rows_all = contract("rm,mcq->rcq", out_cos, moved[:, 0]) - contract(
        "rm,mcq->rcq", out_sin, moved[:, 1]
    )
    rows_all = rows_all * scale_factor
    convolved = lax.all_to_all(rows_all, "ctx", split_axis=0, concat_axis=2, tiled=True)
    return gate * (convolved[0] + skip[:, None] * signal)


def shards(signal, gate, skip, filter_spectrum):
    parts = lax.axis_size("ctx")
    channels, length = signal.shape
    if channels % parts == 0 and 2 * length == LANES * LANES:
        return by_channel(signal, gate, skip, filter_spectrum)
    return by_frequency(signal, gate, skip, filter_spectrum)


def solution(mesh):
    return jax.shard_map(
        shards,
        mesh=mesh,
        in_specs=(P("ch", "ctx"), P("ch", "ctx"), P("ch"), P("ctx", None, "ch", None)),
        out_specs=P("ch", "ctx"),
        check_vma=False,
    )
```

```python
import functools
import math

import jax
import jax.numpy as jnp
import numpy as np
from jax import lax
from jax.experimental import pallas as pl
from jax.experimental.pallas import tpu as pltpu
from jax.sharding import PartitionSpec as P

LANES = 128
HALF = LANES // 2


def split_pair(values):
    high = values.astype(jnp.bfloat16)
    low = (values - high.astype(jnp.float32)).astype(jnp.bfloat16)
    return high, low


def split_table(table):
    table = np.asarray(table, np.float32)
    high = table.astype(jnp.bfloat16)
    low = (table - high.astype(np.float32)).astype(jnp.bfloat16)
    return np.stack([high, low])


def multiply(left, right, dims):
    def dot(a, b):
        return lax.dot_general(a, b, (dims, ((), ())), preferred_element_type=jnp.float32)

    return dot(left[0], right[0]) + (dot(left[0], right[1]) + dot(left[1], right[0]))


ROWS_COLS = ((1,), (0,))
COLS_COLS = ((0,), (0,))


@functools.lru_cache(maxsize=None)
def tables(parts, blocks):
    freq_rows = 2 * parts
    period = freq_rows * blocks
    full_len = period * LANES
    rows = np.arange(parts * blocks)
    index = np.zeros((parts, blocks), np.int64)
    for owner in range(parts):
        for place in range(blocks):
            if owner:
                index[owner, place] = freq_rows * place + owner
            elif place < blocks // 2:
                index[owner, place] = freq_rows * place
            else:
                index[owner, place] = freq_rows * place + parts
    index = index.reshape(-1)
    angle = 2 * np.pi * ((index[:, None] * rows[None, :]) % period) / period
    wave_re, wave_im = np.cos(angle), -np.sin(angle)
    wave_im[0] = np.where(rows % 2 == 0, 1.0, -1.0)
    outer = np.concatenate([wave_re, wave_im], axis=0)
    lane = np.arange(LANES)
    turn = 2 * np.pi * ((index[:, None] * lane[None, :]) % full_len) / full_len
    twist = np.stack([np.cos(turn), np.sin(turn)])
    twist[0, 0], twist[1, 0] = 1.0, 0.0
    freq = 2 * (lane % HALF) + lane // HALF
    theta = 2 * np.pi * ((lane[:, None] * freq[None, :]) % LANES) / LANES
    cos, sin = np.cos(theta), np.sin(theta)
    inner = np.block([[cos, -sin], [sin, cos]])
    inner_back = np.block([[cos.T, sin.T], [-sin.T, cos.T]]) / full_len
    upper = lane % HALF >= HALF // 2
    half_theta = 2 * np.pi * ((lane[:, None] * (2 * freq[None, :] + 1)) % (2 * LANES)) / (2 * LANES)
    alternate = np.where(lane % 2 == 0, 1.0, -1.0)
    zero_re, zero_im = np.where(upper, 0.0, cos), np.where(upper, 0.0, -sin)
    zero_re[:, 0], zero_im[:, 0] = 1.0, alternate
    mid_re = np.where(upper, np.cos(half_theta), 0.0)
    mid_im = np.where(upper, -np.sin(half_theta), 0.0)
    edge = np.block([[zero_re, zero_im], [mid_re, mid_im]])
    weight = np.ones(LANES)
    weight[0] = 0.5
    back_re = np.concatenate([(zero_re * weight).T, mid_re.T], axis=1)
    back_im = np.concatenate([(zero_im * weight).T, mid_im.T], axis=1)
    edge_back = np.concatenate([back_re, back_im], axis=0) / full_len
    return {
        "outer": split_table(outer.T),
        "twist": twist.astype(np.float32),
        "inner": split_table(inner),
        "edge": split_table(edge),
        "inner_back": split_table(inner_back),
        "edge_back": split_table(edge_back),
    }


def spread_kernel(device_ref, signal_ref, *refs):
    *out_refs, work_ref = refs
    channels, length = signal_ref.shape
    blocks = length // LANES
    for block in range(blocks):
        work_ref[pl.ds(block, channels, stride=blocks), :] = signal_ref[:, block * LANES : (block + 1) * LANES]
    rows = channels * blocks // len(out_refs)
    for step, out_ref in enumerate(out_refs):
        out_ref[...] = work_ref[part_rows(device_ref, step, rows), :]


def part_rows(device_ref, step, rows):
    return pl.ds(pl.multiple_of((device_ref[0] ^ step) * rows, rows), rows)


def fold_kernel(device_ref, filter_ref, *refs):
    *out_refs, work_ref = refs
    channels = filter_ref.shape[2]
    blocks = filter_ref.shape[3] // LANES
    lane = lax.broadcasted_iota(jnp.int32, (channels, LANES), 1)
    place = lane % HALF
    reverse = LANES - 1 - lane
    negate = jnp.where(place < HALF // 2, LANES - lane, reverse)
    negate_low = jnp.where(place == 0, 0, negate)
    negate_high = jnp.where(place == 0, LANES - HALF // 2 - lane, negate)

    def tile(row, part, block):
        return filter_ref[row, part, :, block * LANES : (block + 1) * LANES]

    def pick(values, where):
        return jnp.take_along_axis(values, where, axis=1)

    def put(part, block, values):
        work_ref[part, pl.ds(block, channels, stride=blocks), :] = values

    @pl.when(device_ref[0] != 0)
    def _():
        for block in range(blocks):
            mirror = blocks - 1 - block
            put(0, block, tile(0, 0, block) + pick(tile(1, 0, mirror), reverse))
            put(1, block, tile(0, 1, block) - pick(tile(1, 1, mirror), reverse))

    @pl.when(device_ref[0] == 0)
    def _():
        for part in range(2):
            sign = 1.0 - 2.0 * part
            for block in range(blocks):
                mirror, wrapped = blocks - 1 - block, (blocks - block) % blocks
                low, low_back = tile(0, part, block), tile(0, part, mirror)
                direct = jnp.where(place < HALF // 2, low, tile(1, part, block))
                back = jnp.where(place < HALF // 2, tile(1, part, mirror), low_back)
                if block < blocks // 2:
                    values = direct + sign * pick(back, negate_low)
                    edge = low + sign * jnp.where(lane == 0, tile(0, part, wrapped), low_back)
                    values = jnp.where(place == 0, edge, values)
                else:
                    direct = jnp.where(place == 0, pltpu.roll(low, LANES - HALF // 2, 1), direct)
                    values = direct + sign * pick(back, negate_high)
                if block == 0 and part == 1:
                    values = jnp.where(lane == 0, 2.0 * tile(0, 0, blocks // 2), values)
                put(part, block, values)

    left = lax.broadcasted_iota(jnp.int32, (blocks, LANES), 1) < HALF
    own = channels // len(out_refs)
    for step, out_ref in enumerate(out_refs):
        for c in range(0, own, 2):
            for part in range(2):
                rows = part_rows(device_ref, step, own * blocks)
                turned = work_ref[part, rows, :][c * blocks : (c + 2) * blocks].T
                first, second = turned[:blocks], turned[blocks:]
                out_ref[c, part] = jnp.where(left, first, pltpu.roll(second, HALF, 1))
                out_ref[c + 1, part] = jnp.where(left, pltpu.roll(first, HALF, 1), second)


def forward_kernel(device_ref, *refs, own):
    *x_refs, outer_ref, twist_ref, inner_ref, edge_ref, out_ref, work_ref = refs
    slots = work_ref.shape[0]
    blocks = slots // len(x_refs)
    for step, x_ref in enumerate(x_refs):
        rows = part_rows(device_ref, step, blocks)
        for c in range(own):
            work_ref[rows, c * LANES : (c + 1) * LANES] = x_ref[c * blocks : (c + 1) * blocks]
    first = multiply((outer_ref[0], outer_ref[1]), split_pair(work_ref[...]), COLS_COLS)
    cos, sin = twist_ref[0], twist_ref[1]
    head = lax.broadcasted_iota(jnp.int32, (8, 2 * LANES), 0) == 0
    for c in range(own):
        re = first[:slots, c * LANES : (c + 1) * LANES]
        im = first[slots:, c * LANES : (c + 1) * LANES]
        turned = jnp.concatenate([re * cos + im * sin, im * cos - re * sin], axis=1)
        pair = split_pair(turned)
        spectrum = multiply(pair, (inner_ref[0], inner_ref[1]), ROWS_COLS)
        edge = multiply((pair[0][:16], pair[1][:16]), (edge_ref[0], edge_ref[1]), ROWS_COLS)
        out_ref[c, 0] = spectrum[:, :LANES]
        out_ref[c, 1] = spectrum[:, LANES:]
        top = jnp.where(head, edge[:8], spectrum[:8])
        out_ref[c, 0, :8] = top[:, :LANES]
        out_ref[c, 1, :8] = top[:, LANES:]


def backward_kernel(device_ref, spectrum_ref, *refs, parts):
    filter_refs, refs = refs[:parts], refs[parts:]
    outer_ref, twist_ref, inner_ref, edge_ref, *out_refs, turned_ref, work_ref = refs
    own, _, slots, _ = spectrum_ref.shape
    blocks = slots // parts
    row = lax.broadcasted_iota(jnp.int32, (blocks, LANES), 0)
    lane = lax.broadcasted_iota(jnp.int32, (blocks, LANES), 1)
    for step in range(parts):
        rows = part_rows(device_ref, step, blocks)
        first = jnp.logical_and(row == 0, (device_ref[0] ^ step) == 0)
        corner = jnp.logical_and(first, lane == 0)
        cos, sin = twist_ref[0, rows, :], twist_ref[1, rows, :]
        pieces = []
        for c in range(own):
            filt_re, filt_im = filter_refs[step][c, 0], filter_refs[step][c, 1]
            re, im = spectrum_ref[c, 0, rows, :], spectrum_ref[c, 1, rows, :]
            low, high = re * filt_re, im * filt_im
            out_re = jnp.where(corner, low, low - high)
            out_im = jnp.where(corner, high, re * filt_im + im * filt_re)
            pieces.append(jnp.concatenate([out_re, out_im], axis=1))
        pair = split_pair(jnp.concatenate(pieces, axis=0))
        back = multiply(pair, (inner_ref[0], inner_ref[1]), ROWS_COLS)
        for c in range(own):
            start = c * blocks
            edge = multiply(
                (pair[0][start : start + 16], pair[1][start : start + 16]), (edge_ref[0], edge_ref[1]), ROWS_COLS
            )
            top = jnp.concatenate([edge, edge[:1] * jnp.zeros((blocks - 16, 1), jnp.float32)], axis=0)
            mine = back[start : start + blocks]
            re = jnp.where(first, top[:, :LANES], mine[:, :LANES])
            im = jnp.where(first, top[:, LANES:], mine[:, LANES:])
            columns = slice(c * LANES, (c + 1) * LANES)
            high, low = split_pair(re * cos - im * sin)
            turned_ref[0, 0, rows, columns] = high
            turned_ref[1, 0, rows, columns] = low
            high, low = split_pair(im * cos + re * sin)
            turned_ref[0, 1, rows, columns] = high
            turned_ref[1, 1, rows, columns] = low
    turned = turned_ref[...].reshape(2, 2 * slots, own * LANES)
    work_ref[...] = multiply((outer_ref[0], outer_ref[1]), (turned[0], turned[1]), ROWS_COLS)
    for step, out_ref in enumerate(out_refs):
        rows = part_rows(device_ref, step, blocks)
        for c in range(own):
            out_ref[c * blocks : (c + 1) * blocks] = work_ref[rows, c * LANES : (c + 1) * LANES]


def finish_kernel(device_ref, *refs):
    *conv_refs, signal_ref, gate_ref, skip_ref, out_ref, work_ref = refs
    channels, length = signal_ref.shape
    blocks = length // LANES
    for step, conv_ref in enumerate(conv_refs):
        work_ref[part_rows(device_ref, step, conv_ref.shape[0]), :] = conv_ref[...]
    skip = skip_ref[...]
    for block in range(blocks):
        where = slice(block * LANES, (block + 1) * LANES)
        conv = work_ref[pl.ds(block, channels, stride=blocks), :]
        out_ref[:, where] = gate_ref[:, where] * (conv + skip * signal_ref[:, where])


def call(kernel, shapes, device, *operands, scratch, limit):
    one = not isinstance(shapes, list)
    shapes = [shapes] if one else shapes
    vmem = pl.BlockSpec(memory_space=pltpu.VMEM)
    result = pl.pallas_call(
        kernel,
        out_shape=[jax.ShapeDtypeStruct(shape, jnp.float32) for shape in shapes],
        in_specs=[pl.BlockSpec(memory_space=pltpu.SMEM)] + [vmem] * len(operands),
        out_specs=[vmem] * len(shapes),
        scratch_shapes=scratch,
        compiler_params=pltpu.CompilerParams(vmem_limit_bytes=limit << 20),
    )(device, *operands)
    return result[0] if one else result


def order_of(parts):
    return sorted(range(1, parts), key=lambda step: -step)


def exchange(blocks):
    parts = len(blocks)
    moved = [None] * parts
    moved[0] = blocks[0]
    for step in order_of(parts):
        moved[step] = lax.ppermute(blocks[step], "ctx", [(one, one ^ step) for one in range(parts)])
    return moved


def by_channel(signal, gate, skip, filter_spectrum):
    parts = lax.axis_size("ctx")
    channels, length = signal.shape
    blocks, own = length // LANES, channels // parts
    slots = parts * blocks
    table = tables(parts, blocks)
    device = lax.axis_index("ctx")[None]
    piece = (own * blocks, LANES)
    whole = pltpu.VMEM((channels * blocks, LANES), jnp.float32)
    spread = call(spread_kernel, [piece] * parts, device, signal, scratch=[whole], limit=8)
    columns = exchange(spread)
    folded = call(
        fold_kernel,
        [(own, 2, blocks, LANES)] * parts,
        device,
        filter_spectrum,
        scratch=[pltpu.VMEM((2, channels * blocks, LANES), jnp.float32)],
        limit=16,
    )
    filt = exchange(folded)
    spectrum = call(
        functools.partial(forward_kernel, own=own),
        (own, 2, slots, LANES),
        device,
        *columns,
        table["outer"],
        table["twist"],
        table["inner"],
        table["edge"],
        scratch=[pltpu.VMEM((slots, own * LANES), jnp.float32)],
        limit=24,
    )
    rows = call(
        functools.partial(backward_kernel, parts=parts),
        [piece] * parts,
        device,
        spectrum,
        *filt,
        table["outer"],
        table["twist"],
        table["inner_back"],
        table["edge_back"],
        scratch=[
            pltpu.VMEM((2, 2, slots, own * LANES), jnp.bfloat16),
            pltpu.VMEM((slots, own * LANES), jnp.float32),
        ],
        limit=24,
    )
    convolved = exchange(rows)
    return call(finish_kernel, signal.shape, device, *convolved, signal, gate, skip[:, None], scratch=[whole], limit=12)


def contract(form, left, right):
    return jnp.einsum(form, left, right, precision=lax.Precision.HIGHEST)


def phase_table(left, right, period):
    angle = left * right % period
    theta = angle.astype(jnp.float32) * (2.0 * math.pi / period)
    return (jnp.cos(theta), jnp.sin(theta))


def product_pair(form, left, right):
    real_part = contract(form, left[0], right[0]) - contract(form, left[1], right[1])
    imag_part = contract(form, left[0], right[1]) + contract(form, left[1], right[0])
    return (real_part, imag_part)


def times_pair(left, right):
    return (left[0] * right[0] - left[1] * right[1], left[0] * right[1] + left[1] * right[0])


def local_tables(length):
    outer_len = 128
    inner_len = length // outer_len
    outer_index = jnp.arange(outer_len, dtype=jnp.int32)
    inner_index = jnp.arange(inner_len, dtype=jnp.int32)
    outer_wave = phase_table(outer_index[:, None], outer_index[None, :], outer_len)
    twist_wave = phase_table(outer_index[:, None], inner_index[None, :], length)
    inner_wave = phase_table(inner_index[:, None], inner_index[None, :], inner_len)
    return (outer_len, inner_len, outer_wave, twist_wave, inner_wave)


def local_forward(values, length):
    outer_len, inner_len, outer_wave, twist_wave, inner_wave = local_tables(length)
    lead_shape = values[0].shape[:-1]
    values = tuple((part.reshape(lead_shape + (outer_len, inner_len)) for part in values))
    values = product_pair("as,...sb->...ab", (outer_wave[0], -outer_wave[1]), values)
    values = times_pair(values, (twist_wave[0], -twist_wave[1]))
    return product_pair("...as,bs->...ab", values, (inner_wave[0], -inner_wave[1]))


def local_inverse(values, length):
    outer_len, inner_len, outer_wave, twist_wave, inner_wave = local_tables(length)
    lead_shape = values[0].shape[:-2]
    values = product_pair("...ak,sk->...as", values, inner_wave)
    values = times_pair(values, twist_wave)
    values = product_pair("ta,...as->...ts", outer_wave, values)
    return tuple((part.reshape(lead_shape + (length,)) for part in values))


def by_frequency(signal, gate, skip, filter_spectrum):
    parts_count = lax.axis_size("ctx")
    freq_rows = 2 * parts_count
    channels, tok_local = signal.shape
    slice_len = tok_local // parts_count
    full_len = freq_rows * tok_local
    device = lax.axis_index("ctx")
    is_first = device == 0
    columns = lax.all_to_all(signal[None], "ctx", split_axis=2, concat_axis=0, tiled=True)
    source_row = jnp.arange(parts_count, dtype=jnp.int32)
    dest_index = jnp.arange(parts_count, dtype=jnp.int32)
    slice_pos = device * slice_len + jnp.arange(slice_len, dtype=jnp.int32)
    upper_freq = jnp.where(dest_index == 0, parts_count, freq_rows - dest_index)
    row_freq = jnp.stack([dest_index, upper_freq], axis=1).reshape(freq_rows)
    spot = jnp.arange(tok_local, dtype=jnp.int32)
    wave_cos, wave_sin = phase_table(row_freq[:, None], source_row[None, :], freq_rows)
    first_re = contract("kr,rcq->kcq", wave_cos, columns)
    first_im = -contract("kr,rcq->kcq", wave_sin, columns)
    twist_cos, twist_sin = phase_table(row_freq[:, None], slice_pos[None, :], full_len)
    first_pair = times_pair((first_re, first_im), (twist_cos[:, None, :], -twist_sin[:, None, :]))
    stacked = jnp.stack(first_pair, axis=1)
    moved = lax.all_to_all(stacked, "ctx", split_axis=0, concat_axis=3, tiled=True)
    low_pair = (moved[0, 0], moved[0, 1])
    high_pair = (moved[1, 0], moved[1, 1])
    rows_pair = (jnp.stack([low_pair[0], high_pair[0]]), jnp.stack([low_pair[1], high_pair[1]]))
    spectral = local_forward(rows_pair, tok_local)
    inner_len = tok_local // 128
    filt = filter_spectrum.reshape(2, 2, channels, inner_len, 128).swapaxes(3, 4)
    product = times_pair(spectral, (filt[:, 0], filt[:, 1]))
    restored = local_inverse(product, tok_local)
    my_freq = jnp.stack([device, jnp.where(is_first, parts_count, freq_rows - device)])
    back_cos, back_sin = phase_table(my_freq[:, None], spot[None, :], full_len)
    turned = times_pair(restored, (back_cos[:, None, :], back_sin[:, None, :]))
    scale_factor = 1.0 / full_len
    stacked = jnp.stack(turned, axis=1)
    moved = lax.all_to_all(stacked, "ctx", split_axis=3, concat_axis=0, tiled=True)
    out_cos, out_sin = phase_table(source_row[:, None], row_freq[None, :], freq_rows)
    rows_all = contract("rm,mcq->rcq", out_cos, moved[:, 0]) - contract(
        "rm,mcq->rcq", out_sin, moved[:, 1]
    )
    rows_all = rows_all * scale_factor
    convolved = lax.all_to_all(rows_all, "ctx", split_axis=0, concat_axis=2, tiled=True)
    return gate * (convolved[0] + skip[:, None] * signal)


def shards(signal, gate, skip, filter_spectrum):
    parts = lax.axis_size("ctx")
    channels, length = signal.shape
    if channels % (2 * parts) == 0 and parts & (parts - 1) == 0 and 2 * length == LANES * LANES:
        return by_channel(signal, gate, skip, filter_spectrum)
    return by_frequency(signal, gate, skip, filter_spectrum)


def solution(mesh):
    return jax.shard_map(
        shards,
        mesh=mesh,
        in_specs=(P("ch", "ctx"), P("ch", "ctx"), P("ch"), P("ctx", None, "ch", None)),
        out_specs=P("ch", "ctx"),
        check_vma=False,
    )
```

```python
import functools
import math

import jax
import jax.numpy as jnp
import numpy as np
from jax import lax
from jax.experimental import pallas as pl
from jax.experimental.pallas import tpu as pltpu
from jax.sharding import PartitionSpec as P


LANES = 128
HALF = LANES // 2


def split_pair(values):
    high = values.astype(jnp.bfloat16)
    low = (values - high.astype(jnp.float32)).astype(jnp.bfloat16)
    return high, low


def split_table(table):
    table = np.asarray(table, np.float32)
    high = table.astype(jnp.bfloat16)
    low = (table - high.astype(np.float32)).astype(jnp.bfloat16)
    return np.stack([high, low])


def multiply(left, right, dims):
    def dot(a, b):
        return lax.dot_general(a, b, (dims, ((), ())), preferred_element_type=jnp.float32)

    return dot(left[0], right[0]) + (dot(left[0], right[1]) + dot(left[1], right[0]))


def multiply_rows(left, right):
    _, rows, depth = left.shape
    both = jnp.dot(left.reshape(2 * rows, depth), right[0], preferred_element_type=jnp.float32)
    cross = jnp.dot(left[0], right[1], preferred_element_type=jnp.float32)
    return both[:rows] + (both[rows:] + cross)


ROWS_COLS = ((1,), (0,))
COLS_COLS = ((0,), (0,))


@functools.lru_cache(maxsize=None)
def tables(parts, blocks):
    freq_rows = 2 * parts
    period = freq_rows * blocks
    full_len = period * LANES
    rows = np.arange(parts * blocks)
    index = np.zeros((parts, blocks), np.int64)
    for owner in range(parts):
        for place in range(blocks):
            if owner:
                index[owner, place] = freq_rows * place + owner
            elif place < blocks // 2:
                index[owner, place] = freq_rows * place
            else:
                index[owner, place] = freq_rows * place + parts
    index = index.reshape(-1)
    angle = 2 * np.pi * ((index[:, None] * rows[None, :]) % period) / period
    wave_re, wave_im = np.cos(angle), -np.sin(angle)
    wave_im[0] = np.where(rows % 2 == 0, 1.0, -1.0)
    outer = np.stack([wave_re.reshape(-1, LANES, rows.size), wave_im.reshape(-1, LANES, rows.size)], axis=1)
    outer = outer.reshape(-1, rows.size)
    lane = np.arange(LANES)
    turn = 2 * np.pi * ((index[:, None] * lane[None, :]) % full_len) / full_len
    twist = np.stack([np.cos(turn), np.sin(turn)])
    twist[0, 0], twist[1, 0] = 1.0, 0.0
    freq = 2 * (lane % HALF) + lane // HALF
    theta = 2 * np.pi * ((lane[:, None] * freq[None, :]) % LANES) / LANES
    cos, sin = np.cos(theta), np.sin(theta)
    inner = np.block([[cos, -sin], [sin, cos]])
    inner_back = np.block([[cos.T, sin.T], [-sin.T, cos.T]]) / full_len
    upper = lane % HALF >= HALF // 2
    half_theta = 2 * np.pi * ((lane[:, None] * (2 * freq[None, :] + 1)) % (2 * LANES)) / (2 * LANES)
    alternate = np.where(lane % 2 == 0, 1.0, -1.0)
    zero_re, zero_im = np.where(upper, 0.0, cos), np.where(upper, 0.0, -sin)
    zero_re[:, 0], zero_im[:, 0] = 1.0, alternate
    mid_re = np.where(upper, np.cos(half_theta), 0.0)
    mid_im = np.where(upper, -np.sin(half_theta), 0.0)
    edge = np.block([[zero_re, zero_im], [mid_re, mid_im]])
    weight = np.ones(LANES)
    weight[0] = 0.5
    back_re = np.concatenate([(zero_re * weight).T, mid_re.T], axis=1)
    back_im = np.concatenate([(zero_im * weight).T, mid_im.T], axis=1)
    edge_back = np.concatenate([back_re, back_im], axis=0) / full_len
    return {
        "outer": split_table(outer.T),
        "twist": twist.astype(np.float32),
        "there": np.concatenate([split_table(inner), split_table(edge)]),
        "back": np.concatenate([split_table(inner_back), split_table(edge_back)]),
    }


def spread_kernel(device_ref, signal_ref, *refs):
    *out_refs, work_ref = refs
    channels, length = signal_ref.shape
    blocks = length // LANES
    for block in range(blocks):
        work_ref[pl.ds(block, channels, stride=blocks), :] = signal_ref[:, block * LANES : (block + 1) * LANES]
    rows = channels * blocks // len(out_refs)
    for step, out_ref in enumerate(out_refs):
        out_ref[...] = work_ref[part_rows(device_ref, step, rows), :]


def part_rows(device_ref, step, rows):
    return pl.ds(pl.multiple_of((device_ref[0] ^ step) * rows, rows), rows)


def fold_kernel(device_ref, filter_ref, *refs):
    *out_refs, work_ref = refs
    channels = filter_ref.shape[2]
    blocks = filter_ref.shape[3] // LANES
    lane = lax.broadcasted_iota(jnp.int32, (channels, LANES), 1)
    place = lane % HALF
    reverse = LANES - 1 - lane
    negate = jnp.where(place < HALF // 2, LANES - lane, reverse)
    negate_low = jnp.where(place == 0, 0, negate)
    negate_high = jnp.where(place == 0, LANES - HALF // 2 - lane, negate)

    def tile(row, part, block):
        return filter_ref[row, part, :, block * LANES : (block + 1) * LANES]

    def pick(values, where):
        return jnp.take_along_axis(values, where, axis=1)

    def put(part, block, values):
        work_ref[part, pl.ds(block, channels, stride=blocks), :] = values

    @pl.when(device_ref[0] != 0)
    def _():
        for block in range(blocks):
            mirror = blocks - 1 - block
            put(0, block, tile(0, 0, block) + pick(tile(1, 0, mirror), reverse))
            put(1, block, tile(0, 1, block) - pick(tile(1, 1, mirror), reverse))

    @pl.when(device_ref[0] == 0)
    def _():
        for part in range(2):
            sign = 1.0 - 2.0 * part
            for block in range(blocks):
                mirror, wrapped = blocks - 1 - block, (blocks - block) % blocks
                low, low_back = tile(0, part, block), tile(0, part, mirror)
                direct = jnp.where(place < HALF // 2, low, tile(1, part, block))
                back = jnp.where(place < HALF // 2, tile(1, part, mirror), low_back)
                if block < blocks // 2:
                    values = direct + sign * pick(back, negate_low)
                    edge = low + sign * jnp.where(lane == 0, tile(0, part, wrapped), low_back)
                    values = jnp.where(place == 0, edge, values)
                else:
                    direct = jnp.where(place == 0, pltpu.roll(low, LANES - HALF // 2, 1), direct)
                    values = direct + sign * pick(back, negate_high)
                if block == 0 and part == 1:
                    values = jnp.where(lane == 0, 2.0 * tile(0, 0, blocks // 2), values)
                put(part, block, values)

    left = lax.broadcasted_iota(jnp.int32, (blocks, LANES), 1) < HALF
    own = channels // len(out_refs)
    for step, out_ref in enumerate(out_refs):
        for c in range(0, own, 2):
            for part in range(2):
                rows = part_rows(device_ref, step, own * blocks)
                turned = work_ref[part, rows, :][c * blocks : (c + 2) * blocks].T
                first, second = turned[:blocks], turned[blocks:]
                out_ref[c, part] = jnp.where(left, first, pltpu.roll(second, HALF, 1))
                out_ref[c + 1, part] = jnp.where(left, pltpu.roll(first, HALF, 1), second)


def forward_kernel(device_ref, *refs, own):
    *x_refs, outer_ref, twist_ref, inner_ref, out_ref, work_ref = refs
    slots = work_ref.shape[0]
    blocks = slots // len(x_refs)
    for step, x_ref in enumerate(x_refs):
        rows = part_rows(device_ref, step, blocks)
        for c in range(own):
            work_ref[rows, c * LANES : (c + 1) * LANES] = x_ref[c * blocks : (c + 1) * blocks]
    first = multiply((outer_ref[0], outer_ref[1]), split_pair(work_ref[...]), COLS_COLS)
    head = lax.broadcasted_iota(jnp.int32, (8, 2 * LANES), 0) == 0
    for c in range(own):
        pieces = []
        for start in range(0, slots, LANES):
            cos, sin = twist_ref[0, start : start + LANES], twist_ref[1, start : start + LANES]
            re = first[2 * start : 2 * start + LANES, c * LANES : (c + 1) * LANES]
            im = first[2 * start + LANES : 2 * start + 2 * LANES, c * LANES : (c + 1) * LANES]
            pieces.append(jnp.concatenate([re * cos + im * sin, im * cos - re * sin], axis=1))
        pair = split_pair(jnp.concatenate(pieces, axis=0))
        spectrum = multiply(pair, (inner_ref[0], inner_ref[1]), ROWS_COLS)
        edge = multiply((pair[0][:16], pair[1][:16]), (inner_ref[2], inner_ref[3]), ROWS_COLS)
        out_ref[c, 0] = spectrum[:, :LANES]
        out_ref[c, 1] = spectrum[:, LANES:]
        top = jnp.where(head, edge[:8], spectrum[:8])
        out_ref[c, 0, :8] = top[:, :LANES]
        out_ref[c, 1, :8] = top[:, LANES:]


def backward_kernel(device_ref, spectrum_ref, *refs, steps, parts):
    filter_refs, (outer_ref, twist_ref, inner_ref, *refs) = refs[: len(steps)], refs[len(steps) :]
    *refs, product_ref = refs
    own, _, slots, _ = spectrum_ref.shape
    blocks = slots // parts
    held = blocks * len(steps)
    row = lax.broadcasted_iota(jnp.int32, (blocks, LANES), 0)
    lane = lax.broadcasted_iota(jnp.int32, (blocks, LANES), 1)
    corner_place = jnp.logical_and(row == 0, lane == 0)
    for index, step in enumerate(steps):
        owner = device_ref[0] ^ step
        rows = part_rows(device_ref, step, blocks)
        place = index // 2 * LANES + (owner & 1) * blocks
        place = pl.ds(pl.multiple_of(place, blocks), blocks)
        corner = jnp.logical_and(corner_place, owner == 0)
        for c in range(own):
            filt_re, filt_im = filter_refs[index][c, 0], filter_refs[index][c, 1]
            re, im = spectrum_ref[c, 0, rows, :], spectrum_ref[c, 1, rows, :]
            low, high = re * filt_re, im * filt_im
            out_re = jnp.where(corner, low, low - high)
            out_im = jnp.where(corner, high, re * filt_im + im * filt_re)
            for level, values in enumerate(split_pair(jnp.concatenate([out_re, out_im], axis=1))):
                product_ref[level, c, place, :] = values
    products = product_ref[...].reshape(2, own * held, 2 * LANES)
    spread = multiply_rows(products, (inner_ref[0], inner_ref[1]))
    starts = range(0, held, LANES)
    tops = [product_ref[:, c, start : start + 16] for c in range(own) for start in starts]
    edges = multiply_rows(jnp.concatenate(tops, axis=1), (inner_ref[2], inner_ref[3]))
    head = lax.broadcasted_iota(jnp.int32, (8, 2 * LANES), 0) == 0
    columns, tables = [], []
    for c in range(own):
        pieces = []
        for index, start in enumerate(starts):
            pair = (device_ref[0] ^ steps[2 * index]) // 2
            rows = pl.ds(pl.multiple_of(pair * LANES, LANES), LANES)
            cos, sin = twist_ref[0, rows, :], twist_ref[1, rows, :]
            back = spread[c * held + start : c * held + start + LANES]
            edge = edges[16 * (c * len(starts) + index) :][:8]
            top = jnp.where(jnp.logical_and(head, pair == 0), edge, back[:8])
            back = jnp.concatenate([top, back[8:]], axis=0)
            re, im = back[:, :LANES], back[:, LANES:]
            pieces += [re * cos - im * sin, im * cos + re * sin]
            if c == 0:
                tables.append(outer_ref[:, :, pl.ds(pl.multiple_of(pair * 2 * LANES, 2 * LANES), 2 * LANES)])
        columns.append(jnp.concatenate(pieces, axis=0))
    turned = split_pair(jnp.concatenate(columns, axis=1))
    total = multiply_rows(jnp.concatenate(tables, axis=2), turned)
    if len(refs) == 1:
        refs[0][...] = total
        return
    sum_ref, *out_refs, work_ref = refs
    work_ref[...] = sum_ref[...] + total
    for step, out_ref in enumerate(out_refs):
        rows = part_rows(device_ref, step, blocks)
        for c in range(own):
            out_ref[c * blocks : (c + 1) * blocks] = work_ref[rows, c * LANES : (c + 1) * LANES]


def split_steps(parts):
    early = [step for step in range(parts) if step & 2 == 0]
    return early, [step for step in range(parts) if step & 2]


def ready_kernel(skip_ref, signal_ref, gate_ref, scale_ref, base_ref):
    channels, length = signal_ref.shape
    row = lax.broadcasted_iota(jnp.int32, (channels, LANES), 0)
    skip = jnp.zeros((channels, LANES), jnp.float32)
    for channel in range(channels):
        skip = jnp.where(row == channel, skip_ref[channel], skip)
    for start in range(0, length, LANES):
        where = slice(start, start + LANES)
        gate = gate_ref[:, where]
        scale_ref[:, where] = gate
        base_ref[:, where] = gate * (skip * signal_ref[:, where])


def finish_kernel(device_ref, *refs):
    *conv_refs, scale_ref, base_ref, out_ref, work_ref = refs
    channels, length = base_ref.shape
    blocks = length // LANES
    for step, conv_ref in enumerate(conv_refs):
        work_ref[part_rows(device_ref, step, conv_ref.shape[0]), :] = conv_ref[...]
    for block in range(blocks):
        where = slice(block * LANES, (block + 1) * LANES)
        conv = work_ref[pl.ds(block, channels, stride=blocks), :]
        out_ref[:, where] = scale_ref[:, where] * conv + base_ref[:, where]


def call(kernel, shapes, device, *operands, scratch, limit):
    one = not isinstance(shapes, list)
    shapes = [shapes] if one else shapes
    vmem = pl.BlockSpec(memory_space=pltpu.VMEM)
    run = pl.pallas_call(
        kernel,
        out_shape=[jax.ShapeDtypeStruct(shape, jnp.float32) for shape in shapes],
        in_specs=[pl.BlockSpec(memory_space=pltpu.SMEM)] + [vmem] * len(operands),
        out_specs=[vmem] * len(shapes),
        scratch_shapes=scratch,
        compiler_params=pltpu.CompilerParams(vmem_limit_bytes=limit << 20),
    )
    result = run(device, *operands)
    return result[0] if one else result


def exchange(blocks):
    parts = len(blocks)
    moved = [None] * parts
    moved[0] = blocks[0]
    for step in range(1, parts):
        moved[step] = lax.ppermute(blocks[step], "ctx", [(one, one ^ step) for one in range(parts)])
    return moved


def by_channel(signal, gate, skip, filter_spectrum):
    parts = lax.axis_size("ctx")
    channels, length = signal.shape
    blocks, own = length // LANES, channels // parts
    slots = parts * blocks
    table = tables(parts, blocks)
    device = lax.axis_index("ctx")[None]
    piece = (own * blocks, LANES)
    whole = pltpu.VMEM((channels * blocks, LANES), jnp.float32)
    spread = call(spread_kernel, [piece] * parts, device, signal, scratch=[whole], limit=4)
    columns = exchange(spread)
    scale, base = call(ready_kernel, [signal.shape] * 2, skip, signal, gate, scratch=[], limit=6)
    folded = call(
        fold_kernel,
        [(own, 2, blocks, LANES)] * parts,
        device,
        filter_spectrum,
        scratch=[pltpu.VMEM((2, channels * blocks, LANES), jnp.float32)],
        limit=10,
    )
    filt = exchange(folded)
    spectrum = call(
        functools.partial(forward_kernel, own=own),
        (own, 2, slots, LANES),
        device,
        *columns,
        table["outer"],
        table["twist"],
        table["there"],
        scratch=[pltpu.VMEM((slots, own * LANES), jnp.float32)],
        limit=12,
    )
    back_tables = (table["outer"], table["twist"], table["back"])
    early, late = split_steps(parts)
    product = pltpu.VMEM((2, own, slots // 2, 2 * LANES), jnp.bfloat16)
    partial = call(
        functools.partial(backward_kernel, steps=early, parts=parts),
        (slots, own * LANES),
        device,
        spectrum,
        *[filt[step] for step in early],
        *back_tables,
        scratch=[product],
        limit=10,
    )
    rows = call(
        functools.partial(backward_kernel, steps=late, parts=parts),
        [piece] * parts,
        device,
        spectrum,
        *[filt[step] for step in late],
        *back_tables,
        partial,
        scratch=[pltpu.VMEM((slots, own * LANES), jnp.float32), product],
        limit=10,
    )
    convolved = exchange(rows)
    return call(finish_kernel, signal.shape, device, *convolved, scale, base, scratch=[whole], limit=6)


def contract(form, left, right):
    return jnp.einsum(form, left, right, precision=lax.Precision.HIGHEST)


def phase_table(left, right, period):
    angle = left * right % period
    theta = angle.astype(jnp.float32) * (2.0 * math.pi / period)
    return (jnp.cos(theta), jnp.sin(theta))


def product_pair(form, left, right):
    real_part = contract(form, left[0], right[0]) - contract(form, left[1], right[1])
    imag_part = contract(form, left[0], right[1]) + contract(form, left[1], right[0])
    return (real_part, imag_part)


def times_pair(left, right):
    return (left[0] * right[0] - left[1] * right[1], left[0] * right[1] + left[1] * right[0])


def local_tables(length):
    outer_len = 128
    inner_len = length // outer_len
    outer_index = jnp.arange(outer_len, dtype=jnp.int32)
    inner_index = jnp.arange(inner_len, dtype=jnp.int32)
    outer_wave = phase_table(outer_index[:, None], outer_index[None, :], outer_len)
    twist_wave = phase_table(outer_index[:, None], inner_index[None, :], length)
    inner_wave = phase_table(inner_index[:, None], inner_index[None, :], inner_len)
    return (outer_len, inner_len, outer_wave, twist_wave, inner_wave)


def local_forward(values, length):
    outer_len, inner_len, outer_wave, twist_wave, inner_wave = local_tables(length)
    lead_shape = values[0].shape[:-1]
    values = tuple((part.reshape(lead_shape + (outer_len, inner_len)) for part in values))
    values = product_pair("as,...sb->...ab", (outer_wave[0], -outer_wave[1]), values)
    values = times_pair(values, (twist_wave[0], -twist_wave[1]))
    return product_pair("...as,bs->...ab", values, (inner_wave[0], -inner_wave[1]))


def local_inverse(values, length):
    _, _, outer_wave, twist_wave, inner_wave = local_tables(length)
    lead_shape = values[0].shape[:-2]
    values = product_pair("...ak,sk->...as", values, inner_wave)
    values = times_pair(values, twist_wave)
    values = product_pair("ta,...as->...ts", outer_wave, values)
    return tuple((part.reshape(lead_shape + (length,)) for part in values))


def by_frequency(signal, gate, skip, filter_spectrum):
    parts_count = lax.axis_size("ctx")
    freq_rows = 2 * parts_count
    channels, tok_local = signal.shape
    slice_len = tok_local // parts_count
    full_len = freq_rows * tok_local
    device = lax.axis_index("ctx")
    is_first = device == 0
    columns = lax.all_to_all(signal[None], "ctx", split_axis=2, concat_axis=0, tiled=True)
    source_row = jnp.arange(parts_count, dtype=jnp.int32)
    dest_index = jnp.arange(parts_count, dtype=jnp.int32)
    slice_pos = device * slice_len + jnp.arange(slice_len, dtype=jnp.int32)
    upper_freq = jnp.where(dest_index == 0, parts_count, freq_rows - dest_index)
    row_freq = jnp.stack([dest_index, upper_freq], axis=1).reshape(freq_rows)
    spot = jnp.arange(tok_local, dtype=jnp.int32)
    wave_cos, wave_sin = phase_table(row_freq[:, None], source_row[None, :], freq_rows)
    first_re = contract("kr,rcq->kcq", wave_cos, columns)
    first_im = -contract("kr,rcq->kcq", wave_sin, columns)
    twist_cos, twist_sin = phase_table(row_freq[:, None], slice_pos[None, :], full_len)
    first_pair = times_pair((first_re, first_im), (twist_cos[:, None, :], -twist_sin[:, None, :]))
    stacked = jnp.stack(first_pair, axis=1)
    moved = lax.all_to_all(stacked, "ctx", split_axis=0, concat_axis=3, tiled=True)
    low_pair = (moved[0, 0], moved[0, 1])
    high_pair = (moved[1, 0], moved[1, 1])
    rows_pair = (jnp.stack([low_pair[0], high_pair[0]]), jnp.stack([low_pair[1], high_pair[1]]))
    spectral = local_forward(rows_pair, tok_local)
    inner_len = tok_local // 128
    filt = filter_spectrum.reshape(2, 2, channels, inner_len, 128).swapaxes(3, 4)
    product = times_pair(spectral, (filt[:, 0], filt[:, 1]))
    restored = local_inverse(product, tok_local)
    my_freq = jnp.stack([device, jnp.where(is_first, parts_count, freq_rows - device)])
    back_cos, back_sin = phase_table(my_freq[:, None], spot[None, :], full_len)
    turned = times_pair(restored, (back_cos[:, None, :], back_sin[:, None, :]))
    scale_factor = 1.0 / full_len
    stacked = jnp.stack(turned, axis=1)
    moved = lax.all_to_all(stacked, "ctx", split_axis=3, concat_axis=0, tiled=True)
    out_cos, out_sin = phase_table(source_row[:, None], row_freq[None, :], freq_rows)
    rows_all = contract("rm,mcq->rcq", out_cos, moved[:, 0]) - contract(
        "rm,mcq->rcq", out_sin, moved[:, 1]
    )
    rows_all = rows_all * scale_factor
    convolved = lax.all_to_all(rows_all, "ctx", split_axis=0, concat_axis=2, tiled=True)
    return gate * (convolved[0] + skip[:, None] * signal)


def shards(signal, gate, skip, filter_spectrum):
    parts = lax.axis_size("ctx")
    channels, length = signal.shape
    if channels % (2 * parts) == 0 and parts & (parts - 1) == 0 and parts >= 4 and 2 * length == LANES * LANES:
        return by_channel(signal, gate, skip, filter_spectrum)
    return by_frequency(signal, gate, skip, filter_spectrum)


def solution(mesh):
    return jax.shard_map(
        shards,
        mesh=mesh,
        in_specs=(P("ch", "ctx"), P("ch", "ctx"), P("ch"), P("ctx", None, "ch", None)),
        out_specs=P("ch", "ctx"),
        check_vma=False,
    )
```

```python
import functools
import math

import jax
import jax.numpy as jnp
import numpy as np
from jax import lax
from jax.experimental import pallas as pl
from jax.experimental.pallas import tpu as pltpu
from jax.sharding import PartitionSpec as P


LANES = 128
HALF = LANES // 2
FINE = 16


def split_pair(values):
    high = values.astype(jnp.bfloat16)
    low = (values - high.astype(jnp.float32)).astype(jnp.bfloat16)
    return high, low


def split_table(table):
    table = np.asarray(table, np.float32)
    high = table.astype(jnp.bfloat16)
    low = (table - high.astype(np.float32)).astype(jnp.bfloat16)
    return np.stack([high, low])


def multiply(left, right, dims):
    def dot(a, b):
        return lax.dot_general(a, b, (dims, ((), ())), preferred_element_type=jnp.float32)

    return dot(left[0], right[0]) + (dot(left[0], right[1]) + dot(left[1], right[0]))


def multiply_rows(left, right):
    _, rows, depth = left.shape
    both = jnp.dot(left.reshape(2 * rows, depth), right[0], preferred_element_type=jnp.float32)
    cross = jnp.dot(left[0], right[1], preferred_element_type=jnp.float32)
    return both[:rows] + (both[rows:] + cross)


ROWS_COLS = ((1,), (0,))
COLS_COLS = ((0,), (0,))


@functools.lru_cache(maxsize=None)
def tables(parts, blocks):
    freq_rows = 2 * parts
    period = freq_rows * blocks
    full_len = period * LANES
    index = np.zeros((parts, blocks), np.int64)
    for owner in range(parts):
        for place in range(blocks):
            if owner:
                index[owner, place] = freq_rows * place + owner
            elif place < blocks // 2:
                index[owner, place] = freq_rows * place
            else:
                index[owner, place] = freq_rows * place + parts
    index = index.reshape(-1)

    def wave(rows):
        angle = 2 * np.pi * ((rows[:, None] * index[None, :]) % period) / period
        return np.cos(angle), np.sin(angle)

    def paired(re, im):
        return np.stack([re.reshape(len(re), -1, LANES), im.reshape(len(im), -1, LANES)], axis=2).reshape(len(re), -1)

    coarse_rows, fine_rows = np.arange(0, parts * blocks, FINE), np.arange(FINE)
    (coarse_cos, coarse_sin), (fine_cos, fine_sin) = wave(coarse_rows), wave(fine_rows)
    coarse = np.stack([paired(coarse_cos, -coarse_sin), paired(-coarse_sin, -coarse_cos)])
    fine = np.stack([paired(fine_cos, fine_cos), paired(fine_sin, fine_sin)])
    coarse[0, :, LANES], coarse[1, :, LANES] = 1.0, 0.0
    fine[0, :, LANES] = np.where(fine_rows % 2 == 0, 1.0, -1.0)
    lane = np.arange(LANES)

    def turn(rows):
        angle = 2 * np.pi * ((rows[:, None] * lane[None, :]) % full_len) / full_len
        return np.stack([np.cos(angle), np.sin(angle)])

    freq = 2 * (lane % HALF) + lane // HALF
    theta = 2 * np.pi * ((lane[:, None] * freq[None, :]) % LANES) / LANES
    cos, sin = np.cos(theta), np.sin(theta)
    inner = np.block([[cos, -sin], [sin, cos]])
    inner_back = np.block([[cos.T, sin.T], [-sin.T, cos.T]]) / full_len
    upper = lane % HALF >= HALF // 2
    half_theta = 2 * np.pi * ((lane[:, None] * (2 * freq[None, :] + 1)) % (2 * LANES)) / (2 * LANES)
    alternate = np.where(lane % 2 == 0, 1.0, -1.0)
    zero_re, zero_im = np.where(upper, 0.0, cos), np.where(upper, 0.0, -sin)
    zero_re[:, 0], zero_im[:, 0] = 1.0, alternate
    mid_re = np.where(upper, np.cos(half_theta), 0.0)
    mid_im = np.where(upper, -np.sin(half_theta), 0.0)
    edge = np.block([[zero_re, zero_im], [mid_re, mid_im]])
    weight = np.ones(LANES)
    weight[0] = 0.5
    back_re = np.concatenate([(zero_re * weight).T, mid_re.T], axis=1)
    back_im = np.concatenate([(zero_im * weight).T, mid_im.T], axis=1)
    edge_back = np.concatenate([back_re, back_im], axis=0) / full_len
    return {
        "coarse": coarse.astype(np.float32),
        "fine": fine.astype(np.float32),
        "place": turn(freq_rows * np.arange(blocks)).astype(np.float32),
        "owner": turn(np.arange(parts + 1)).astype(np.float32),
        "there": np.concatenate([split_table(inner), split_table(edge)]),
        "back": np.concatenate([split_table(inner_back), split_table(edge_back)]),
    }


def table_kernel(coarse_ref, fine_ref, place_ref, owner_ref, outer_ref, twist_ref):
    for index in range(coarse_ref.shape[1]):
        rows = slice(index * FINE, (index + 1) * FINE)
        values = coarse_ref[0, index : index + 1] * fine_ref[0] + coarse_ref[1, index : index + 1] * fine_ref[1]
        for level, piece in enumerate(split_pair(values)):
            outer_ref[level, rows] = piece
    blocks, parts = place_ref.shape[1], owner_ref.shape[1] - 1
    cos, sin = place_ref[0], place_ref[1]
    for owner in range(1, parts + 1):
        step_cos, step_sin = owner_ref[0, owner : owner + 1], owner_ref[1, owner : owner + 1]
        both = (cos * step_cos - sin * step_sin, sin * step_cos + cos * step_sin)
        for part, values in enumerate(both):
            if owner < parts:
                twist_ref[part, owner * blocks : (owner + 1) * blocks] = values
            else:
                twist_ref[part, blocks // 2 : blocks] = values[blocks // 2 :]
                twist_ref[part, : blocks // 2] = place_ref[part, : blocks // 2]


def spread_kernel(device_ref, signal_ref, *refs):
    *out_refs, work_ref = refs
    channels, length = signal_ref.shape
    blocks = length // LANES
    for block in range(blocks):
        work_ref[pl.ds(block, channels, stride=blocks), :] = signal_ref[:, block * LANES : (block + 1) * LANES]
    rows = channels * blocks // len(out_refs)
    for step, out_ref in enumerate(out_refs):
        out_ref[...] = work_ref[part_rows(device_ref, step, rows), :]


def part_rows(device_ref, step, rows):
    return pl.ds(pl.multiple_of((device_ref[0] ^ step) * rows, rows), rows)


def fold_kernel(device_ref, filter_ref, *refs):
    *out_refs, work_ref = refs
    channels = filter_ref.shape[2]
    blocks = filter_ref.shape[3] // LANES
    lane = lax.broadcasted_iota(jnp.int32, (channels, LANES), 1)
    place = lane % HALF
    reverse = LANES - 1 - lane
    negate = jnp.where(place < HALF // 2, LANES - lane, reverse)
    negate_low = jnp.where(place == 0, 0, negate)
    negate_high = jnp.where(place == 0, LANES - HALF // 2 - lane, negate)

    def tile(row, part, block):
        return filter_ref[row, part, :, block * LANES : (block + 1) * LANES]

    def pick(values, where):
        return jnp.take_along_axis(values, where, axis=1)

    def put(part, block, values):
        work_ref[part, pl.ds(block, channels, stride=blocks), :] = values

    @pl.when(device_ref[0] != 0)
    def _():
        for block in range(blocks):
            mirror = blocks - 1 - block
            put(0, block, tile(0, 0, block) + pick(tile(1, 0, mirror), reverse))
            put(1, block, tile(0, 1, block) - pick(tile(1, 1, mirror), reverse))

    @pl.when(device_ref[0] == 0)
    def _():
        for part in range(2):
            sign = 1.0 - 2.0 * part
            for block in range(blocks):
                mirror, wrapped = blocks - 1 - block, (blocks - block) % blocks
                low, low_back = tile(0, part, block), tile(0, part, mirror)
                direct = jnp.where(place < HALF // 2, low, tile(1, part, block))
                back = jnp.where(place < HALF // 2, tile(1, part, mirror), low_back)
                if block < blocks // 2:
                    values = direct + sign * pick(back, negate_low)
                    edge = low + sign * jnp.where(lane == 0, tile(0, part, wrapped), low_back)
                    values = jnp.where(place == 0, edge, values)
                else:
                    direct = jnp.where(place == 0, pltpu.roll(low, LANES - HALF // 2, 1), direct)
                    values = direct + sign * pick(back, negate_high)
                if block == 0 and part == 1:
                    values = jnp.where(lane == 0, 2.0 * tile(0, 0, blocks // 2), values)
                put(part, block, values)

    left = lax.broadcasted_iota(jnp.int32, (blocks, LANES), 1) < HALF
    own = channels // len(out_refs)
    for step, out_ref in enumerate(out_refs):
        for c in range(0, own, 2):
            for part in range(2):
                rows = part_rows(device_ref, step, own * blocks)
                turned = work_ref[part, rows, :][c * blocks : (c + 2) * blocks].T
                first, second = turned[:blocks], turned[blocks:]
                out_ref[c, part] = jnp.where(left, first, pltpu.roll(second, HALF, 1))
                out_ref[c + 1, part] = jnp.where(left, pltpu.roll(first, HALF, 1), second)


def forward_kernel(device_ref, *refs, own):
    *x_refs, outer_ref, twist_ref, inner_ref, out_ref, work_ref = refs
    slots = work_ref.shape[0]
    blocks = slots // len(x_refs)
    for step, x_ref in enumerate(x_refs):
        rows = part_rows(device_ref, step, blocks)
        for c in range(own):
            work_ref[rows, c * LANES : (c + 1) * LANES] = x_ref[c * blocks : (c + 1) * blocks]
    first = multiply((outer_ref[0], outer_ref[1]), split_pair(work_ref[...]), COLS_COLS)
    head = lax.broadcasted_iota(jnp.int32, (8, 2 * LANES), 0) == 0
    for c in range(own):
        pieces = []
        for start in range(0, slots, LANES):
            cos, sin = twist_ref[0, start : start + LANES], twist_ref[1, start : start + LANES]
            re = first[2 * start : 2 * start + LANES, c * LANES : (c + 1) * LANES]
            im = first[2 * start + LANES : 2 * start + 2 * LANES, c * LANES : (c + 1) * LANES]
            pieces.append(jnp.concatenate([re * cos + im * sin, im * cos - re * sin], axis=1))
        pair = split_pair(jnp.concatenate(pieces, axis=0))
        spectrum = multiply(pair, (inner_ref[0], inner_ref[1]), ROWS_COLS)
        edge = multiply((pair[0][:16], pair[1][:16]), (inner_ref[2], inner_ref[3]), ROWS_COLS)
        out_ref[c, 0] = spectrum[:, :LANES]
        out_ref[c, 1] = spectrum[:, LANES:]
        top = jnp.where(head, edge[:8], spectrum[:8])
        out_ref[c, 0, :8] = top[:, :LANES]
        out_ref[c, 1, :8] = top[:, LANES:]


def backward_kernel(device_ref, spectrum_ref, *refs, steps, parts):
    filter_refs, (outer_ref, twist_ref, inner_ref, *refs) = refs[: len(steps)], refs[len(steps) :]
    *refs, product_ref = refs
    own, _, slots, _ = spectrum_ref.shape
    blocks = slots // parts
    held = blocks * len(steps)
    row = lax.broadcasted_iota(jnp.int32, (blocks, LANES), 0)
    lane = lax.broadcasted_iota(jnp.int32, (blocks, LANES), 1)
    corner_place = jnp.logical_and(row == 0, lane == 0)
    for index, step in enumerate(steps):
        owner = device_ref[0] ^ step
        rows = part_rows(device_ref, step, blocks)
        place = index // 2 * LANES + (owner & 1) * blocks
        place = pl.ds(pl.multiple_of(place, blocks), blocks)
        corner = jnp.logical_and(corner_place, owner == 0)
        for c in range(own):
            filt_re, filt_im = filter_refs[index][c, 0], filter_refs[index][c, 1]
            re, im = spectrum_ref[c, 0, rows, :], spectrum_ref[c, 1, rows, :]
            low, high = re * filt_re, im * filt_im
            out_re = jnp.where(corner, low, low - high)
            out_im = jnp.where(corner, high, re * filt_im + im * filt_re)
            for level, values in enumerate(split_pair(jnp.concatenate([out_re, out_im], axis=1))):
                product_ref[level, c, place, :] = values
    products = product_ref[...].reshape(2, own * held, 2 * LANES)
    spread = multiply_rows(products, (inner_ref[0], inner_ref[1]))
    starts = range(0, held, LANES)
    tops = [product_ref[:, c, start : start + 16] for c in range(own) for start in starts]
    edges = multiply_rows(jnp.concatenate(tops, axis=1), (inner_ref[2], inner_ref[3]))
    head = lax.broadcasted_iota(jnp.int32, (8, 2 * LANES), 0) == 0
    columns, tables = [], []
    for c in range(own):
        pieces = []
        for index, start in enumerate(starts):
            pair = (device_ref[0] ^ steps[2 * index]) // 2
            rows = pl.ds(pl.multiple_of(pair * LANES, LANES), LANES)
            cos, sin = twist_ref[0, rows, :], twist_ref[1, rows, :]
            back = spread[c * held + start : c * held + start + LANES]
            edge = edges[16 * (c * len(starts) + index) :][:8]
            top = jnp.where(jnp.logical_and(head, pair == 0), edge, back[:8])
            back = jnp.concatenate([top, back[8:]], axis=0)
            re, im = back[:, :LANES], back[:, LANES:]
            pieces += [re * cos - im * sin, im * cos + re * sin]
            if c == 0:
                tables.append(outer_ref[:, :, pl.ds(pl.multiple_of(pair * 2 * LANES, 2 * LANES), 2 * LANES)])
        columns.append(jnp.concatenate(pieces, axis=0))
    turned = split_pair(jnp.concatenate(columns, axis=1))
    total = multiply_rows(jnp.concatenate(tables, axis=2), turned)
    if len(refs) == 1:
        refs[0][...] = total
        return
    sum_ref, *out_refs, work_ref = refs
    work_ref[...] = sum_ref[...] + total
    for step, out_ref in enumerate(out_refs):
        rows = part_rows(device_ref, step, blocks)
        for c in range(own):
            out_ref[c * blocks : (c + 1) * blocks] = work_ref[rows, c * LANES : (c + 1) * LANES]


def split_steps(parts):
    early = [step for step in range(parts) if step & 2 == 0]
    return early, [step for step in range(parts) if step & 2]


def ready_kernel(skip_ref, signal_ref, gate_ref, scale_ref, base_ref):
    channels, length = signal_ref.shape
    row = lax.broadcasted_iota(jnp.int32, (channels, LANES), 0)
    skip = jnp.zeros((channels, LANES), jnp.float32)
    for channel in range(channels):
        skip = jnp.where(row == channel, skip_ref[channel], skip)
    for start in range(0, length, LANES):
        where = slice(start, start + LANES)
        gate = gate_ref[:, where]
        scale_ref[:, where] = gate
        base_ref[:, where] = gate * (skip * signal_ref[:, where])


def finish_kernel(device_ref, *refs):
    *conv_refs, scale_ref, base_ref, out_ref, work_ref = refs
    channels, length = base_ref.shape
    blocks = length // LANES
    for step, conv_ref in enumerate(conv_refs):
        work_ref[part_rows(device_ref, step, conv_ref.shape[0]), :] = conv_ref[...]
    for block in range(blocks):
        where = slice(block * LANES, (block + 1) * LANES)
        conv = work_ref[pl.ds(block, channels, stride=blocks), :]
        out_ref[:, where] = scale_ref[:, where] * conv + base_ref[:, where]


def call(kernel, shapes, *operands, scratch, limit, scalars=1):
    one = not isinstance(shapes, list)
    shapes = [shapes] if one else shapes
    shapes = [shape if hasattr(shape, "dtype") else jax.ShapeDtypeStruct(shape, jnp.float32) for shape in shapes]
    vmem, smem = pl.BlockSpec(memory_space=pltpu.VMEM), pl.BlockSpec(memory_space=pltpu.SMEM)
    run = pl.pallas_call(
        kernel,
        out_shape=shapes,
        in_specs=[smem] * scalars + [vmem] * (len(operands) - scalars),
        out_specs=[vmem] * len(shapes),
        scratch_shapes=scratch,
        compiler_params=pltpu.CompilerParams(vmem_limit_bytes=limit << 20),
    )
    result = run(*operands)
    return result[0] if one else result


def exchange(blocks):
    parts = len(blocks)
    moved = [None] * parts
    moved[0] = blocks[0]
    for step in range(1, parts):
        moved[step] = lax.ppermute(blocks[step], "ctx", [(one, one ^ step) for one in range(parts)])
    return moved


def by_channel(signal, gate, skip, filter_spectrum):
    parts = lax.axis_size("ctx")
    channels, length = signal.shape
    blocks, own = length // LANES, channels // parts
    slots = parts * blocks
    table = tables(parts, blocks)
    device = lax.axis_index("ctx")[None]
    piece = (own * blocks, LANES)
    whole = pltpu.VMEM((channels * blocks, LANES), jnp.float32)
    spread = call(spread_kernel, [piece] * parts, device, signal, scratch=[whole], limit=4)
    columns = exchange(spread)
    scale, base = call(ready_kernel, [signal.shape] * 2, skip, signal, gate, scratch=[], limit=6)
    folded = call(
        fold_kernel,
        [(own, 2, blocks, LANES)] * parts,
        device,
        filter_spectrum,
        scratch=[pltpu.VMEM((2, channels * blocks, LANES), jnp.float32)],
        limit=10,
    )
    filt = exchange(folded)
    outer, twist = call(
        table_kernel,
        [jax.ShapeDtypeStruct((2, slots, 2 * slots), jnp.bfloat16), (2, slots, LANES)],
        table["coarse"],
        table["fine"],
        table["place"],
        table["owner"],
        scratch=[],
        limit=8,
        scalars=0,
    )
    spectrum = call(
        functools.partial(forward_kernel, own=own),
        (own, 2, slots, LANES),
        device,
        *columns,
        outer,
        twist,
        table["there"],
        scratch=[pltpu.VMEM((slots, own * LANES), jnp.float32)],
        limit=12,
    )
    back_tables = (outer, twist, table["back"])
    early, late = split_steps(parts)
    product = pltpu.VMEM((2, own, slots // 2, 2 * LANES), jnp.bfloat16)
    partial = call(
        functools.partial(backward_kernel, steps=early, parts=parts),
        (slots, own * LANES),
        device,
        spectrum,
        *[filt[step] for step in early],
        *back_tables,
        scratch=[product],
        limit=10,
    )
    rows = call(
        functools.partial(backward_kernel, steps=late, parts=parts),
        [piece] * parts,
        device,
        spectrum,
        *[filt[step] for step in late],
        *back_tables,
        partial,
        scratch=[pltpu.VMEM((slots, own * LANES), jnp.float32), product],
        limit=10,
    )
    convolved = exchange(rows)
    return call(finish_kernel, signal.shape, device, *convolved, scale, base, scratch=[whole], limit=6)


def contract(form, left, right):
    return jnp.einsum(form, left, right, precision=lax.Precision.HIGHEST)


def phase_table(left, right, period):
    angle = left * right % period
    theta = angle.astype(jnp.float32) * (2.0 * math.pi / period)
    return (jnp.cos(theta), jnp.sin(theta))


def product_pair(form, left, right):
    real_part = contract(form, left[0], right[0]) - contract(form, left[1], right[1])
    imag_part = contract(form, left[0], right[1]) + contract(form, left[1], right[0])
    return (real_part, imag_part)


def times_pair(left, right):
    return (left[0] * right[0] - left[1] * right[1], left[0] * right[1] + left[1] * right[0])


def local_tables(length):
    outer_len = 128
    inner_len = length // outer_len
    outer_index = jnp.arange(outer_len, dtype=jnp.int32)
    inner_index = jnp.arange(inner_len, dtype=jnp.int32)
    outer_wave = phase_table(outer_index[:, None], outer_index[None, :], outer_len)
    twist_wave = phase_table(outer_index[:, None], inner_index[None, :], length)
    inner_wave = phase_table(inner_index[:, None], inner_index[None, :], inner_len)
    return (outer_len, inner_len, outer_wave, twist_wave, inner_wave)


def local_forward(values, length):
    outer_len, inner_len, outer_wave, twist_wave, inner_wave = local_tables(length)
    lead_shape = values[0].shape[:-1]
    values = tuple((part.reshape(lead_shape + (outer_len, inner_len)) for part in values))
    values = product_pair("as,...sb->...ab", (outer_wave[0], -outer_wave[1]), values)
    values = times_pair(values, (twist_wave[0], -twist_wave[1]))
    return product_pair("...as,bs->...ab", values, (inner_wave[0], -inner_wave[1]))


def local_inverse(values, length):
    _, _, outer_wave, twist_wave, inner_wave = local_tables(length)
    lead_shape = values[0].shape[:-2]
    values = product_pair("...ak,sk->...as", values, inner_wave)
    values = times_pair(values, twist_wave)
    values = product_pair("ta,...as->...ts", outer_wave, values)
    return tuple((part.reshape(lead_shape + (length,)) for part in values))


def by_frequency(signal, gate, skip, filter_spectrum):
    parts_count = lax.axis_size("ctx")
    freq_rows = 2 * parts_count
    channels, tok_local = signal.shape
    slice_len = tok_local // parts_count
    full_len = freq_rows * tok_local
    device = lax.axis_index("ctx")
    is_first = device == 0
    columns = lax.all_to_all(signal[None], "ctx", split_axis=2, concat_axis=0, tiled=True)
    source_row = jnp.arange(parts_count, dtype=jnp.int32)
    dest_index = jnp.arange(parts_count, dtype=jnp.int32)
    slice_pos = device * slice_len + jnp.arange(slice_len, dtype=jnp.int32)
    upper_freq = jnp.where(dest_index == 0, parts_count, freq_rows - dest_index)
    row_freq = jnp.stack([dest_index, upper_freq], axis=1).reshape(freq_rows)
    spot = jnp.arange(tok_local, dtype=jnp.int32)
    wave_cos, wave_sin = phase_table(row_freq[:, None], source_row[None, :], freq_rows)
    first_re = contract("kr,rcq->kcq", wave_cos, columns)
    first_im = -contract("kr,rcq->kcq", wave_sin, columns)
    twist_cos, twist_sin = phase_table(row_freq[:, None], slice_pos[None, :], full_len)
    first_pair = times_pair((first_re, first_im), (twist_cos[:, None, :], -twist_sin[:, None, :]))
    stacked = jnp.stack(first_pair, axis=1)
    moved = lax.all_to_all(stacked, "ctx", split_axis=0, concat_axis=3, tiled=True)
    low_pair = (moved[0, 0], moved[0, 1])
    high_pair = (moved[1, 0], moved[1, 1])
    rows_pair = (jnp.stack([low_pair[0], high_pair[0]]), jnp.stack([low_pair[1], high_pair[1]]))
    spectral = local_forward(rows_pair, tok_local)
    inner_len = tok_local // 128
    filt = filter_spectrum.reshape(2, 2, channels, inner_len, 128).swapaxes(3, 4)
    product = times_pair(spectral, (filt[:, 0], filt[:, 1]))
    restored = local_inverse(product, tok_local)
    my_freq = jnp.stack([device, jnp.where(is_first, parts_count, freq_rows - device)])
    back_cos, back_sin = phase_table(my_freq[:, None], spot[None, :], full_len)
    turned = times_pair(restored, (back_cos[:, None, :], back_sin[:, None, :]))
    scale_factor = 1.0 / full_len
    stacked = jnp.stack(turned, axis=1)
    moved = lax.all_to_all(stacked, "ctx", split_axis=3, concat_axis=0, tiled=True)
    out_cos, out_sin = phase_table(source_row[:, None], row_freq[None, :], freq_rows)
    rows_all = contract("rm,mcq->rcq", out_cos, moved[:, 0]) - contract(
        "rm,mcq->rcq", out_sin, moved[:, 1]
    )
    rows_all = rows_all * scale_factor
    convolved = lax.all_to_all(rows_all, "ctx", split_axis=0, concat_axis=2, tiled=True)
    return gate * (convolved[0] + skip[:, None] * signal)


def shards(signal, gate, skip, filter_spectrum):
    parts = lax.axis_size("ctx")
    channels, length = signal.shape
    if channels % (2 * parts) == 0 and parts & (parts - 1) == 0 and parts >= 4 and 2 * length == LANES * LANES:
        return by_channel(signal, gate, skip, filter_spectrum)
    return by_frequency(signal, gate, skip, filter_spectrum)


def solution(mesh):
    return jax.shard_map(
        shards,
        mesh=mesh,
        in_specs=(P("ch", "ctx"), P("ch", "ctx"), P("ch"), P("ctx", None, "ch", None)),
        out_specs=P("ch", "ctx"),
        check_vma=False,
    )
```
